32 devices in a mesh: tok: 4 (over x, core), kv: 8 (over z, y).
Axes of the slice: x: 2, y: 2, z: 4, core: 2. Of those that a mesh axis runs over, the one named last changes fastest.
Arguments:
- queries: bfloat16 [4096, 768], P(('tok', 'kv')), may hold values from -36 to 36
- new_kv: bfloat16 [4096, 256], P(('tok', 'kv')), may hold values from -6 to 6
- segment_ids: int32 [4096], P(('tok', 'kv')), may hold values from 0 to 63, as said below
- prefix_len: int32 [64], P(('tok', 'kv')), may hold values from 0 to 4096, as said below
- page_table: int32 [32, 32], P(('tok', 'kv')), may hold values from 0 to 31, as said below
- cache: bfloat16 [1024, 128, 256], P(('tok', 'kv')), may hold values from -6 to 6
Outputs:
- attention: bfloat16 [4096, 768], P(('tok', 'kv'))
The draws below stay inside these ranges and needn't reach their ends.
Inputs may be any that keep to these rules, and one draw needn't show every extreme that they name: `segment_ids`: device d's rows hold segments d * 2 to d * 2 + 1 in order, each on one row or more. Over each device's segments, the sum of ceil(prefix_len / 128) is at most 32; some device reaches it in every draw. page_table[d, k] for k // 8 = r lies in [r * 8, (r + 1) * 8); each such block of a row is a permutation of it; entries past the device's used pages are unused.
All inputs are finite; a program needn't handle non-finite values.
Results may differ from the reference program's by a relative error of at most 0.0085.
Values may be sent and summed in bfloat16 or wider, within the bound.
No kernel may reach another device: no remote copies, remote signals or barrier semaphores. Data moves between devices by JAX's collectives and lax.ppermute only.
A program may use at most 64 MiB of HBM per device.

```python
import jax
import jax.numpy as jnp
from jax import lax

HD = 128
HEADS = 6
PAGE = 128
SEG_DEV = 2
REACH = 4
TOK_DEV = 128
PPO = 8
POOL = 32
TOKENS = 4096
SEGS = 64
DEVICES = 32


def joint_tokens(key):
    base_key = jax.random.fold_in(key, 11)
    query_key, pair_key = jax.random.split(base_key)
    query_rows = jnp.clip(jax.random.normal(query_key, (TOKENS, HEADS, HD), jnp.float32), -6.0, 6.0)
    pair_rows = jnp.clip(jax.random.normal(pair_key, (TOKENS, 2, HD), jnp.float32), -6.0, 6.0)
    return (query_rows.reshape(TOKENS, HEADS * HD), pair_rows.reshape(TOKENS, 2 * HD))


def draw_queries(key, part):
    query_rows, pair_rows = joint_tokens(key)
    return query_rows.astype(jnp.bfloat16)


def draw_new_kv(key, part):
    query_rows, pair_rows = joint_tokens(key)
    return pair_rows.astype(jnp.bfloat16)


def draw_segment_ids(key, part):
    base_key = jax.random.fold_in(key, 31)
    ranking = jax.random.randint(base_key, (DEVICES, TOK_DEV - 1), 0, 1 << 20)
    ranking = ranking * TOK_DEV + jnp.arange(TOK_DEV - 1)[None, :]
    ordering = jnp.argsort(ranking, axis=1)
    cut_rows = jnp.sort(ordering[:, :SEG_DEV - 1] + 1, axis=1)
    row_order = jnp.arange(TOK_DEV)
    local_seg = jnp.sum((row_order[None, :, None] >= cut_rows[:, None, :]).astype(jnp.int32), axis=2)
    first_seg = jnp.arange(DEVICES)[:, None] * SEG_DEV
    return (first_seg + local_seg).reshape(TOKENS).astype(jnp.int32)


def page_layout(key):
    base_key = jax.random.fold_in(key, 47)
    total_key, forced_key, cut_key, offset_key, slot_key = jax.random.split(base_key, 5)
    page_total = REACH * PPO
    used_pages = jax.random.randint(total_key, (DEVICES,), page_total // 4, page_total + 1)
    forced = jax.random.randint(forced_key, (), 0, DEVICES)
    is_forced = jnp.arange(DEVICES) == forced
    used_pages = jnp.where(is_forced, page_total, used_pages)
    raw_cuts = jax.random.randint(cut_key, (DEVICES, SEG_DEV - 1), 0, page_total + 1)
    cut_pages = jnp.sort(jnp.minimum(raw_cuts, used_pages[:, None]), axis=1)
    cut_pages = jnp.where(is_forced[:, None], used_pages[:, None], cut_pages)
    bounds = jnp.concatenate([jnp.zeros((DEVICES, 1), jnp.int32), cut_pages, used_pages[:, None]], axis=1)
    page_count = bounds[:, 1:] - bounds[:, :-1]
    offset = jax.random.randint(offset_key, (DEVICES, SEG_DEV), 0, PAGE)
    offset = jnp.where(is_forced[:, None], 0, offset)
    lengths = jnp.maximum(page_count * PAGE - offset, 0)
    ranking = jax.random.randint(slot_key, (DEVICES, REACH, PPO), 0, 1 << 20) * PPO + jnp.arange(PPO)[None, None, :]
    shuffled = jnp.argsort(ranking, axis=2)
    table_rows = shuffled + (jnp.arange(REACH) * PPO)[None, :, None]
    return (lengths.reshape(SEGS).astype(jnp.int32), table_rows.reshape(DEVICES, REACH * PPO).astype(jnp.int32))


def draw_prefix_len(key, part):
    lengths, table_rows = page_layout(key)
    return lengths


def draw_page_table(key, part):
    lengths, table_rows = page_layout(key)
    return table_rows


def block_scale(own_key, shape, shards, smallest, largest):
    loudness, own = 1.0, jax.random.fold_in(own_key, 6)
    for axis_at, parts in shards:
        heights = jnp.exp(jax.random.uniform(jax.random.fold_in(own, axis_at), (parts,), jnp.float32, smallest / len(shards), largest / len(shards)))
        loudness = loudness * jnp.repeat(heights, shape[axis_at] // parts).reshape([-1 if axis == axis_at else 1 for axis in range(len(shape))])
    return loudness


def normal_values(rng, extent, spread, reach, cuts=(), kind=jnp.bfloat16):
    drawn = spread * jax.random.normal(rng, extent, jnp.float32)
    if cuts:
        drawn = drawn * block_scale(rng, extent, cuts, -0.22, 0.18)
    return jnp.clip(drawn, -reach, reach).astype(kind)


def setup_inputs(seed: int = 0) -> dict:
    splits = jax.random.split(jax.random.key(seed), 7)
    queries = draw_queries(jax.random.fold_in(splits[6], 71), 0)
    new_kv = draw_new_kv(jax.random.fold_in(splits[6], 71), 0)
    segment_ids = draw_segment_ids(jax.random.fold_in(splits[6], 71), 0)
    prefix_len = draw_prefix_len(jax.random.fold_in(splits[6], 71), 0)
    page_table = draw_page_table(jax.random.fold_in(splits[6], 71), 0)
    cache = normal_values(splits[5], (DEVICES * POOL, PAGE, 2 * HD), 1.0, 6.0, ((0, 32),))
    return dict(queries=queries, new_kv=new_kv, segment_ids=segment_ids, prefix_len=prefix_len, page_table=page_table, cache=cache)


def reference(queries, new_kv, segment_ids, prefix_len, page_table, cache):
    page_total = REACH * PPO
    query_all = queries.reshape(DEVICES, TOK_DEV, HEADS, HD)
    pair_all = new_kv.reshape(DEVICES, TOK_DEV, 2 * HD)
    segment_all = segment_ids.reshape(DEVICES, TOK_DEV)
    length_all = prefix_len.reshape(DEVICES, SEG_DEV)
    home_list = jnp.arange(DEVICES, dtype=jnp.int32)

    def one_home(packed):
        home_index, query_rows, pair_rows, segment, length, table_row = packed
        local_seg = segment - home_index * SEG_DEV
        page_count = (length + PAGE - 1) // PAGE
        page_ends = jnp.cumsum(page_count)
        page_starts = page_ends - page_count
        page_number = jnp.arange(page_total, dtype=jnp.int32)
        page_seg = jnp.sum((page_number[:, None] >= page_ends[None, :]).astype(jnp.int32), axis=1)
        clipped = jnp.minimum(page_seg, SEG_DEV - 1).astype(jnp.int32)
        first_page = page_starts[clipped]
        page_limit = jnp.where(page_seg < SEG_DEV, length[clipped], 0)
        positions = ((page_number - first_page) * PAGE)[:, None] + jnp.arange(PAGE, dtype=jnp.int32)[None, :]
        usable = positions < page_limit[:, None]
        owner_index = (home_index + page_number // PPO) % DEVICES
        slot_index = (owner_index * POOL + table_row).astype(jnp.int32)
        cached = cache[slot_index].reshape(page_total * PAGE, 2 * HD)
        key_seg = jnp.repeat(page_seg, PAGE)
        prefix_mask = (local_seg[:, None] == key_seg[None, :]) & usable.reshape(page_total * PAGE)[None, :]
        row_order = jnp.arange(TOK_DEV, dtype=jnp.int32)
        new_mask = (local_seg[:, None] == local_seg[None, :]) & (row_order[None, :] <= row_order[:, None])
        key_mask = jnp.concatenate([prefix_mask, new_mask], axis=1)
        key_rows = jnp.concatenate([cached, pair_rows], axis=0).astype(jnp.float32)
        scores = jnp.einsum("rhd,kd->rhk", query_rows.astype(jnp.float32), key_rows[:, :HD]) * (HD ** -0.5)
        scores = jnp.where(key_mask[:, None, :], scores, -jnp.inf)
        weights = jax.nn.softmax(scores, axis=2).astype(jnp.bfloat16)
        weights = lax.optimization_barrier(weights)
        attended = jnp.einsum("rhk,kd->rhd", weights.astype(jnp.float32), key_rows[:, HD:])
        return attended.reshape(TOK_DEV, HEADS * HD).astype(jnp.bfloat16)

    attention = lax.map(one_home, (home_list, query_all, pair_all, segment_all, length_all, page_table))
    return attention.reshape(TOKENS, HEADS * HD)
```

```python
import functools

import jax
import jax.numpy as jnp
from jax import lax
from jax.experimental import pallas as pl
from jax.experimental.pallas import tpu as pltpu
from jax.sharding import PartitionSpec as P

HD = 128
HEADS = 6
PAGE = 128
REACH = 4
PPO = 8
LONG = 1
ROWS = 128
WIDTH = HEADS * HD
STAT_ROWS = 8
NEGATIVE = -1e30
SCALE2 = HD**-0.5 * 1.4426950408889634
AXES = ("tok", "kv")
CUT, PARITY = REACH, REACH + 1


def iota(axis, shape=(ROWS, PAGE)):
    return lax.broadcasted_iota(jnp.int32, shape, axis)


def fact(q_ref, tile):
    return q_ref[ROWS:, tile * PAGE : (tile + 1) * PAGE].astype(jnp.float32)


def block_keys(q_ref, pages, block):
    row, lane = iota(0).astype(jnp.float32), iota(1).astype(jnp.float32)
    first = row < fact(q_ref, CUT)[:1]
    counts = fact(q_ref, block)
    bias = []
    for slot in range(PPO):
        count = counts[slot : slot + 1]
        bias.append(jnp.where(lane < jnp.where(first, count, -count), 0.0, NEGATIVE))
    flat = pages[...].reshape(PPO * PAGE, 2 * HD)
    return flat[:, :HD], flat[:, HD:], jnp.concatenate(bias, 1)


def pack_kernel(length_hbm, table_hbm, segment_hbm, q_hbm, cache_hbm, out_ref, swap_ref, lengths, table, segments, sems):
    ends = [
        (segment_hbm, segments),
        (length_hbm, lengths),
        (table_hbm, table),
        (q_hbm, out_ref.at[:ROWS]),
        (cache_hbm.at[PPO : 2 * PPO], swap_ref),
    ]
    copies = [pltpu.make_async_copy(source, target, sems.at[i]) for i, (source, target) in enumerate(ends)]
    for copy in copies:
        copy.start()
    odd = jnp.bitwise_and(lax.axis_index("kv"), 1)
    odd = jnp.full((STAT_ROWS, PAGE), odd, jnp.int32).astype(jnp.float32)
    out_ref[ROWS:, PARITY * PAGE : (PARITY + 1) * PAGE] = odd.astype(jnp.bfloat16)
    for copy in copies[:3]:
        copy.wait()
    last = jnp.int32(0)
    for bit in (64, 32, 16, 8, 4, 2, 1):
        last = jnp.where(segments[last + bit] == segments[0], last + bit, last)
    cut = jnp.full((STAT_ROWS, PAGE), last + 1, jnp.int32).astype(jnp.float32)
    out_ref[ROWS:, CUT * PAGE : (CUT + 1) * PAGE] = cut.astype(jnp.bfloat16)
    count0 = lax.shift_right_logical(lengths[0] + (PAGE - 1), 7)
    slot_row = iota(0, (STAT_ROWS, PAGE))
    for block in range(REACH):
        tile = jnp.zeros((STAT_ROWS, PAGE), jnp.int32)
        for k in range(block * PPO, (block + 1) * PPO):
            left0 = jnp.clip(lengths[0] - k * PAGE, 0, PAGE)
            left1 = jnp.clip(lengths[1] - (k - count0) * PAGE, 0, PAGE)
            left = jnp.where(k < count0, left0, -left1)
            tile = jnp.where(slot_row == jnp.bitwise_and(table[0, k], PPO - 1), left, tile)
        out_ref[ROWS:, block * PAGE : (block + 1) * PAGE] = tile.astype(jnp.float32).astype(jnp.bfloat16)
    for copy in copies[3:]:
        copy.wait()


def attend(query, keys, values, bias):
    s = lax.dot_general(query, keys, (((1,), (1,)), ((), ())), preferred_element_type=jnp.float32)
    s = s * SCALE2 + bias
    top = jnp.max(s, axis=1, keepdims=True)
    w = jnp.exp2(s - top)
    total = jnp.sum(w, axis=1, keepdims=True)
    out = jnp.dot(w.astype(jnp.bfloat16), values, preferred_element_type=jnp.float32)
    return out, top, total


def join(a, b):
    top = jnp.maximum(a[1], b[1])
    fa, fb = jnp.exp2(a[1] - top), jnp.exp2(b[1] - top)
    return a[0] * fa + b[0] * fb, top, a[2] * fa + b[2] * fb


def head(x, h):
    return x[:ROWS, h * HD : (h + 1) * HD]


def columns(cols):
    lane = iota(1)
    out = jnp.zeros((ROWS, PAGE), jnp.float32)
    for i, col in enumerate(cols):
        out = jnp.where(lane == i, col, out)
    return out


def write_payload(out_ref, parts):
    for h, (o, top, total) in enumerate(parts):
        out_ref[:ROWS, h * HD : (h + 1) * HD] = (o / total).astype(jnp.bfloat16)
    lse = columns([top + jnp.log2(total) for _, top, total in parts]).T[:STAT_ROWS]
    left = lse
    for i in range(3):
        term = left.astype(jnp.bfloat16)
        out_ref[ROWS:, i * HD : (i + 1) * HD] = term
        left = left - term.astype(jnp.float32)
    out_ref[ROWS:, 3 * HD :] = jnp.zeros((STAT_ROWS, WIDTH - 3 * HD), jnp.bfloat16)


def write_partial(out_ref, lse_ref, parts):
    for h, (o, _, total) in enumerate(parts):
        out_ref[:, h * HD : (h + 1) * HD] = o / total
    lse_ref[...] = columns([top + jnp.log2(total) for _, top, total in parts])


def payload_lse(ref):
    lse = jnp.zeros((STAT_ROWS, PAGE), jnp.float32)
    for i in (2, 1, 0):
        lse = lse + ref[ROWS:, i * HD : (i + 1) * HD].astype(jnp.float32)
    full = jnp.concatenate([lse, jnp.zeros((ROWS - STAT_ROWS, PAGE), jnp.float32)], 0)
    return full.T


def block_parts(q_ref, pages, block):
    keys, values, bias = block_keys(q_ref, pages, block)
    return [attend(head(q_ref, h), keys, values, bias) for h in range(HEADS)]


def near_kernel(q_ref, kv_ref, page_ref, out_ref, lse_ref):
    keys, values, bias = block_keys(q_ref, page_ref, 0)
    row, lane = iota(0), iota(1)
    cut = fact(q_ref, CUT)[:1]
    same = (lane <= row) & ((lane.astype(jnp.float32) >= cut) | (row.astype(jnp.float32) < cut))
    keys = jnp.concatenate([kv_ref[:, :HD], keys], 0)
    values = jnp.concatenate([kv_ref[:, HD:], values], 0)
    bias = jnp.concatenate([jnp.where(same, 0.0, NEGATIVE), bias], 1)
    write_partial(out_ref, lse_ref, [attend(head(q_ref, h), keys, values, bias) for h in range(HEADS)])


def far_kernel(q_ref, page_ref, out_ref):
    write_payload(out_ref, block_parts(q_ref, page_ref, 3))


def middle_kernel(q_ref, page_ref, out_ref, lse_ref):
    write_partial(out_ref, lse_ref, block_parts(q_ref, page_ref, 2))


def swap_parts(parity, q_ref, swap_ref, part_ref, part_lse_ref):
    keys, values, bias = block_keys(q_ref, swap_ref, 1)
    bias = bias + jnp.where(fact(q_ref, PARITY)[:1, :1] == parity, 0.0, NEGATIVE)
    parts = []
    for h in range(HEADS):
        part = part_ref[:, h * HD : (h + 1) * HD], part_lse_ref[:, h : h + 1], 1.0
        parts.append(join(part, attend(head(q_ref, h), keys, values, bias)))
    return parts


def both_kernel(q_ref, swap_ref, part_ref, part_lse_ref, out_ref):
    write_payload(out_ref, swap_parts(1.0, q_ref, swap_ref, part_ref, part_lse_ref))


def own_kernel(q_ref, swap_ref, part_ref, part_lse_ref, out_ref, lse_ref):
    write_partial(out_ref, lse_ref, swap_parts(0.0, q_ref, swap_ref, part_ref, part_lse_ref))


def final_kernel(own_ref, own_lse_ref, two_ref, three_ref, out_ref):
    refs = (own_ref, two_ref, three_ref)
    lses = [own_lse_ref[...], payload_lse(two_ref), payload_lse(three_ref)]
    top = functools.reduce(jnp.maximum, lses)
    shares = [jnp.exp2(x - top) for x in lses]
    total = sum(shares)
    shares = [x / total for x in shares]
    for h in range(HEADS):
        span = slice(h * HD, (h + 1) * HD)
        out = 0.0
        for ref, share in zip(refs, shares):
            out = out + ref[:ROWS, span].astype(jnp.float32) * share[:, h : h + 1]
        out_ref[:, span] = out.astype(jnp.bfloat16)


SMEM = pl.BlockSpec(memory_space=pltpu.SMEM)
VMEM = pl.BlockSpec(memory_space=pltpu.VMEM)


FULL = jax.ShapeDtypeStruct((ROWS, WIDTH), jnp.float32)
LSE = jax.ShapeDtypeStruct((ROWS, PAGE), jnp.float32)
SENT = jax.ShapeDtypeStruct((ROWS + STAT_ROWS, WIDTH), jnp.bfloat16)
RESULT = jax.ShapeDtypeStruct((ROWS, WIDTH), jnp.bfloat16)


def cost(keys):
    return pl.CostEstimate(
        flops=4 * ROWS * HEADS * keys * HD,
        bytes_accessed=4 * keys * HD + 4 * ROWS * WIDTH,
        transcendentals=ROWS * HEADS * keys,
    )


PARAMS = pltpu.CompilerParams(vmem_limit_bytes=16 << 20)


def call(body, name, keys, out_shape, *arrays):
    return pl.pallas_call(
        body,
        in_specs=[VMEM] * len(arrays),
        out_specs=jax.tree.map(lambda _: VMEM, out_shape),
        out_shape=out_shape,
        compiler_params=PARAMS,
        cost_estimate=cost(keys),
        name=name,
    )(*arrays)


def shift(value, steps, count):
    return lax.ppermute(value, AXES, [(s, (s + steps) % count) for s in range(count)])


def after(value, *others):
    return lax.optimization_barrier((value, *others))[0]


def per_device(queries, new_kv, segment_ids, prefix_len, page_table, cache):
    count = lax.axis_size(AXES)
    packed, sent1 = pl.pallas_call(
        pack_kernel,
        in_specs=[pl.BlockSpec(memory_space=pltpu.HBM)] * 5,
        out_specs=[VMEM, VMEM],
        out_shape=[SENT, jax.ShapeDtypeStruct((PPO, PAGE, 2 * HD), jnp.bfloat16)],
        scratch_shapes=[
            pltpu.SMEM(prefix_len.shape, jnp.int32),
            pltpu.SMEM(page_table.shape, jnp.int32),
            pltpu.SMEM(segment_ids.shape, jnp.int32),
            pltpu.SemaphoreType.DMA((5,)),
        ],
        compiler_params=pltpu.CompilerParams(vmem_limit_bytes=(65536 - 1700) << 10),
        cost_estimate=cost(16),
        name="pack",
    )(prefix_len, page_table, segment_ids, queries, cache)
    q3 = shift(packed, 3, count)
    q2 = shift(packed, 2, count)
    swapped = lax.ppermute(sent1, AXES, [(s, s ^ 1) for s in range(count)])
    pool = after(cache, packed)
    blocks = [pool[i * PPO : (i + 1) * PPO] for i in range(REACH)]

    two = call(middle_kernel, "middle", 1024 * LONG, (FULL, LSE), q2, blocks[2])
    far = call(far_kernel, "far", 1024 * LONG, SENT, q3, after(blocks[3], two[1]))
    back3 = shift(far, -3, count)
    both = call(both_kernel, "both", 1024, SENT, q2, after(swapped, far), *two)
    back2 = shift(both, -2, count)
    near = call(near_kernel, "near", 1152, (FULL, LSE), packed, new_kv, blocks[0])
    own = call(own_kernel, "own", 1024, (FULL, LSE), packed, swapped, *near)
    return call(final_kernel, "final", 16, RESULT, *own, back2, back3)


def solution(mesh):
    placed = (
        P(AXES, None),
        P(AXES, None),
        P(AXES),
        P(AXES),
        P(AXES, None),
        P(AXES, None, None),
    )
    return jax.shard_map(per_device, mesh=mesh, in_specs=placed, out_specs=P(AXES, None), check_vma=False)
```

```python
import functools

import jax
import jax.numpy as jnp
from jax import lax
from jax.experimental import pallas as pl
from jax.experimental.pallas import tpu as pltpu
from jax.sharding import PartitionSpec as P

HD = 128
HEADS = 6
PAGE = 128
REACH = 4
PPO = 8
FAR = 8
GROUP = 2
ROWS = 128
WIDTH = HEADS * HD
STAT_ROWS = 8
NEGATIVE = -1e30
SCALE2 = HD**-0.5 * 1.4426950408889634
AXES = ("tok", "kv")
CUT, PARITY = REACH, REACH + 1


def iota(axis, shape=(ROWS, PAGE)):
    return lax.broadcasted_iota(jnp.int32, shape, axis)


def fact(q_ref, tile):
    return q_ref[ROWS:, tile * PAGE : (tile + 1) * PAGE].astype(jnp.float32)


def segment_lanes(q_ref):
    cut = fact(q_ref, CUT)[:1]
    row, lane = iota(0).astype(jnp.float32), iota(1)
    low = jnp.where(lane == 0, 0.0, cut)
    high = jnp.where(lane == 0, cut, jnp.where(lane == 1, float(ROWS), 0.0))
    return jnp.where((row >= low) & (row < high), 1.0, 0.0).astype(jnp.bfloat16)


def block_keys(q_ref, pages, block, skip=None):
    row, lane = iota(0).astype(jnp.float32), iota(1)
    counts = fact(q_ref, block)
    if skip is not None:
        counts = jnp.where(skip, 0.0, counts)
    keys, values = [], []
    ones = jnp.ones((PAGE, PAGE), jnp.bfloat16)
    for slot in range(PPO):
        count = counts[slot : slot + 1]
        count = jnp.where(lane[:1] == 0, count, jnp.where(lane[:1] == 1, -count, float(PAGE)))
        bias = jnp.where(row < count, 0.0, NEGATIVE).astype(jnp.bfloat16)
        page = pages[slot]
        keys.append(jnp.concatenate([page[:, :HD], bias], 1))
        values.append(jnp.concatenate([page[:, HD:], ones], 1))
    return jnp.concatenate(keys, 0), jnp.concatenate(values, 0)


def pack_kernel(length_hbm, table_hbm, segment_hbm, q_hbm, cache_hbm, out_ref, swap_ref, lengths, table, segments, sems):
    ends = [
        (segment_hbm, segments),
        (length_hbm, lengths),
        (table_hbm, table),
        (q_hbm, out_ref.at[:ROWS]),
        (cache_hbm.at[PPO : 2 * PPO], swap_ref),
    ]
    copies = [pltpu.make_async_copy(source, target, sems.at[i]) for i, (source, target) in enumerate(ends)]
    for copy in copies:
        copy.start()
    odd = jnp.bitwise_and(lax.axis_index("kv"), 1)
    odd = jnp.full((STAT_ROWS, PAGE), odd, jnp.int32).astype(jnp.float32)
    out_ref[ROWS:, PARITY * PAGE : (PARITY + 1) * PAGE] = odd.astype(jnp.bfloat16)
    for copy in copies[:3]:
        copy.wait()
    last = jnp.int32(0)
    for bit in (64, 32, 16, 8, 4, 2, 1):
        last = jnp.where(segments[last + bit] == segments[0], last + bit, last)
    cut = jnp.full((STAT_ROWS, PAGE), last + 1, jnp.int32).astype(jnp.float32)
    out_ref[ROWS:, CUT * PAGE : (CUT + 1) * PAGE] = cut.astype(jnp.bfloat16)
    count0 = lax.shift_right_logical(lengths[0] + (PAGE - 1), 7)
    slot_row = iota(0, (STAT_ROWS, PAGE))
    for block in range(REACH):
        tile = jnp.zeros((STAT_ROWS, PAGE), jnp.int32)
        for k in range(block * PPO, (block + 1) * PPO):
            left0 = jnp.clip(lengths[0] - k * PAGE, 0, PAGE)
            left1 = jnp.clip(lengths[1] - (k - count0) * PAGE, 0, PAGE)
            left = jnp.where(k < count0, left0, -left1)
            tile = jnp.where(slot_row == jnp.bitwise_and(table[0, k], PPO - 1), left, tile)
        out_ref[ROWS:, block * PAGE : (block + 1) * PAGE] = tile.astype(jnp.float32).astype(jnp.bfloat16)
    for copy in copies[3:]:
        copy.wait()


def scores(query, keys):
    return lax.dot_general(query, keys, (((1,), (1,)), ((), ())), preferred_element_type=jnp.float32)


def attend(q_ref, keys, values):
    lanes = segment_lanes(q_ref)

    def group_scores(start):
        query = [jnp.concatenate([head(q_ref, h), lanes], 1) for h in range(start, start + GROUP)]
        return scores(jnp.concatenate(query, 0), keys)

    parts = []
    later = group_scores(0)
    for start in range(0, HEADS, GROUP):
        s = later
        if start + GROUP < HEADS:
            later = group_scores(start + GROUP)
        top = jnp.max(s, axis=1, keepdims=True)
        w = jnp.exp2((s - top) * SCALE2).astype(jnp.bfloat16)
        out = jnp.dot(w, values, preferred_element_type=jnp.float32)
        for i in range(GROUP):
            rows = slice(i * ROWS, (i + 1) * ROWS)
            parts.append((out[rows, :HD], top[rows] * SCALE2, out[rows, HD:]))
    return parts


def join(a, b):
    top = jnp.maximum(a[1], b[1])
    fa, fb = jnp.exp2(a[1] - top), jnp.exp2(b[1] - top)
    return a[0] * fa + b[0] * fb, top, a[2] * fa + b[2] * fb


def head(x, h):
    return x[:ROWS, h * HD : (h + 1) * HD]


def columns(cols):
    lane = iota(1)
    out = jnp.zeros((ROWS, PAGE), jnp.float32)
    for i, col in enumerate(cols):
        out = jnp.where(lane == i, col, out)
    return out


def write_payload(out_ref, parts):
    for h, (o, top, total) in enumerate(parts):
        out_ref[:ROWS, h * HD : (h + 1) * HD] = (o / total).astype(jnp.bfloat16)
    lse = columns([top + jnp.log2(total[:, :1]) for _, top, total in parts]).T[:STAT_ROWS]
    left = lse
    for i in range(3):
        term = left.astype(jnp.bfloat16)
        out_ref[ROWS:, i * HD : (i + 1) * HD] = term
        left = left - term.astype(jnp.float32)
    out_ref[ROWS:, 3 * HD :] = jnp.zeros((STAT_ROWS, WIDTH - 3 * HD), jnp.bfloat16)


def write_partial(out_ref, lse_ref, parts):
    for h, (o, _, total) in enumerate(parts):
        out_ref[:, h * HD : (h + 1) * HD] = o / total
    lse_ref[...] = columns([top + jnp.log2(total[:, :1]) for _, top, total in parts])


def payload_lse(ref):
    lse = jnp.zeros((STAT_ROWS, PAGE), jnp.float32)
    for i in (2, 1, 0):
        lse = lse + ref[ROWS:, i * HD : (i + 1) * HD].astype(jnp.float32)
    full = jnp.concatenate([lse, jnp.zeros((ROWS - STAT_ROWS, PAGE), jnp.float32)], 0)
    return full.T


def near_kernel(q_ref, kv_ref, page_ref, out_ref, lse_ref):
    row, lane = iota(0), iota(1)
    cut = fact(q_ref, CUT)[:1]
    same = (lane <= row) & ((lane.astype(jnp.float32) >= cut) | (row.astype(jnp.float32) < cut))
    bias = jnp.where(same, 0.0, NEGATIVE)
    parts = attend(q_ref, *block_keys(q_ref, page_ref, 0))
    values = jnp.concatenate([kv_ref[:, HD:], jnp.ones((ROWS, HD), jnp.bfloat16)], 1)
    for h in range(HEADS):
        s = scores(head(q_ref, h), kv_ref[:, :HD]) + bias
        top = jnp.max(s, axis=1, keepdims=True)
        w = jnp.exp2((s - top) * SCALE2).astype(jnp.bfloat16)
        out = jnp.dot(w, values, preferred_element_type=jnp.float32)
        parts[h] = join(parts[h], (out[:, :HD], top * SCALE2, out[:, HD:]))
    write_partial(out_ref, lse_ref, parts)


def far_kernel(q_ref, page_ref, out_ref):
    write_payload(out_ref, attend(q_ref, *block_keys(q_ref, page_ref, 3)))


def swap_parts(parity, q_ref, swap_ref, part_ref, part_lse_ref):
    parts = attend(q_ref, *block_keys(q_ref, swap_ref, 1, fact(q_ref, PARITY) != parity))
    given = [(part_ref[:, h * HD : (h + 1) * HD], part_lse_ref[:, h : h + 1], 1.0) for h in range(HEADS)]
    return [join(a, b) for a, b in zip(given, parts)]


def middle_kernel(q_ref, page_ref, swap_ref, out_ref):
    pages = block_keys(q_ref, page_ref, 2)
    swapped = block_keys(q_ref, swap_ref, 1, fact(q_ref, PARITY) == 0.0)
    write_payload(out_ref, attend(q_ref, *(jnp.concatenate(both, 0) for both in zip(pages, swapped))))


def own_kernel(q_ref, swap_ref, part_ref, part_lse_ref, out_ref, lse_ref):
    write_partial(out_ref, lse_ref, swap_parts(0.0, q_ref, swap_ref, part_ref, part_lse_ref))


def final_kernel(own_ref, own_lse_ref, two_ref, three_ref, out_ref):
    refs = (own_ref, two_ref, three_ref)
    lses = [own_lse_ref[...], payload_lse(two_ref), payload_lse(three_ref)]
    top = functools.reduce(jnp.maximum, lses)
    shares = [jnp.exp2(x - top) for x in lses]
    total = sum(shares)
    shares = [x / total for x in shares]
    for h in range(HEADS):
        span = slice(h * HD, (h + 1) * HD)
        out = 0.0
        for ref, share in zip(refs, shares):
            out = out + ref[:ROWS, span].astype(jnp.float32) * share[:, h : h + 1]
        out_ref[:, span] = out.astype(jnp.bfloat16)


SMEM = pl.BlockSpec(memory_space=pltpu.SMEM)
VMEM = pl.BlockSpec(memory_space=pltpu.VMEM)


FULL = jax.ShapeDtypeStruct((ROWS, WIDTH), jnp.float32)
LSE = jax.ShapeDtypeStruct((ROWS, PAGE), jnp.float32)
SENT = jax.ShapeDtypeStruct((ROWS + STAT_ROWS, WIDTH), jnp.bfloat16)
RESULT = jax.ShapeDtypeStruct((ROWS, WIDTH), jnp.bfloat16)


def cost(keys):
    return pl.CostEstimate(
        flops=4 * ROWS * HEADS * keys * HD,
        bytes_accessed=4 * keys * HD + 4 * ROWS * WIDTH,
        transcendentals=ROWS * HEADS * keys,
    )


PARAMS = pltpu.CompilerParams(vmem_limit_bytes=16 << 20)


def call(body, name, keys, out_shape, *arrays):
    return pl.pallas_call(
        body,
        in_specs=[VMEM] * len(arrays),
        out_specs=jax.tree.map(lambda _: VMEM, out_shape),
        out_shape=out_shape,
        compiler_params=PARAMS,
        cost_estimate=cost(keys),
        name=name,
    )(*arrays)


def shift(value, steps, count):
    return lax.ppermute(value, AXES, [(s, (s + steps) % count) for s in range(count)])


def after(value, *others):
    return lax.optimization_barrier((value, *others))[0]


def per_device(queries, new_kv, segment_ids, prefix_len, page_table, cache):
    count = lax.axis_size(AXES)
    packed, sent1 = pl.pallas_call(
        pack_kernel,
        in_specs=[pl.BlockSpec(memory_space=pltpu.HBM)] * 5,
        out_specs=[VMEM, VMEM],
        out_shape=[SENT, jax.ShapeDtypeStruct((PPO, PAGE, 2 * HD), jnp.bfloat16)],
        scratch_shapes=[
            pltpu.SMEM(prefix_len.shape, jnp.int32),
            pltpu.SMEM(page_table.shape, jnp.int32),
            pltpu.SMEM(segment_ids.shape, jnp.int32),
            pltpu.SemaphoreType.DMA((5,)),
        ],
        compiler_params=pltpu.CompilerParams(vmem_limit_bytes=16 << 20),
        cost_estimate=cost(16),
        name="pack",
    )(*(pltpu.with_memory_space_constraint(x, pltpu.HBM) for x in (prefix_len, page_table, segment_ids, queries, cache)))
    q3 = shift(packed, 3, count)
    swapped = lax.ppermute(sent1, AXES, [(s, s ^ 1) for s in range(count)])
    q2 = shift(after(packed, packed), 2, count)
    pool = after(cache, packed)
    blocks = [pool[i * PPO : (i + 1) * PPO] for i in range(REACH)]

    far = call(far_kernel, "far", 1024 * FAR, SENT, q3, blocks[3])
    back3 = shift(far, -3, count)
    middle = call(middle_kernel, "middle", 2048, SENT, q2, blocks[2], after(swapped, far))
    back2 = shift(middle, -2, count)
    near = call(near_kernel, "near", 1152, (FULL, LSE), packed, new_kv, blocks[0])
    own = call(own_kernel, "own", 1024, (FULL, LSE), packed, swapped, *near)
    return call(final_kernel, "final", 16, RESULT, *own, back2, back3)


def solution(mesh):
    placed = (
        P(AXES, None),
        P(AXES, None),
        P(AXES),
        P(AXES),
        P(AXES, None),
        P(AXES, None, None),
    )
    return jax.shard_map(per_device, mesh=mesh, in_specs=placed, out_specs=P(AXES, None), check_vma=False)
```

```python
import functools

import jax
import jax.numpy as jnp
from jax import lax
from jax.experimental import pallas as pl
from jax.experimental.pallas import tpu as pltpu
from jax.sharding import PartitionSpec as P

HD = 128
HEADS = 6
PAGE = 128
REACH = 4
PPO = 8
FAR = 2
GROUP = 2
ROWS = 128
WIDTH = HEADS * HD
STAT_ROWS = 8
NEGATIVE = -1e30
SCALE2 = HD**-0.5 * 1.4426950408889634
AXES = ("tok", "kv")
CUT, PARITY = REACH, REACH + 1


def iota(axis, shape=(ROWS, PAGE)):
    return lax.broadcasted_iota(jnp.int32, shape, axis)


def fact(q_ref, tile):
    return q_ref[ROWS:, tile * PAGE : (tile + 1) * PAGE].astype(jnp.float32)


def segment_lanes(q_ref):
    cut = fact(q_ref, CUT)[:1]
    row, lane = iota(0).astype(jnp.float32), iota(1)
    low = jnp.where(lane == 0, 0.0, cut)
    high = jnp.where(lane == 0, cut, jnp.where(lane == 1, float(ROWS), 0.0))
    return jnp.where((row >= low) & (row < high), 1.0, 0.0).astype(jnp.bfloat16)


def block_keys(q_ref, pages, block, skip=None):
    row, lane = iota(0).astype(jnp.float32), iota(1)
    counts = fact(q_ref, block)
    if skip is not None:
        counts = jnp.where(skip, 0.0, counts)
    keys, values = [], []
    ones = jnp.ones((PAGE, PAGE), jnp.bfloat16)
    for slot in range(PPO):
        count = counts[slot : slot + 1]
        count = jnp.where(lane[:1] == 0, count, jnp.where(lane[:1] == 1, -count, float(PAGE)))
        bias = jnp.where(row < count, 0.0, NEGATIVE).astype(jnp.bfloat16)
        page = pages[slot]
        keys.append(jnp.concatenate([page[:, :HD], bias], 1))
        values.append(jnp.concatenate([page[:, HD:], ones], 1))
    return jnp.concatenate(keys, 0), jnp.concatenate(values, 0)


def pack_kernel(length_hbm, table_hbm, segment_hbm, q_hbm, cache_hbm, out_ref, swap_ref, lengths, table, segments, sems):
    ends = [
        (segment_hbm, segments),
        (length_hbm, lengths),
        (table_hbm, table),
        (q_hbm, out_ref.at[:ROWS]),
        (cache_hbm.at[PPO : 2 * PPO], swap_ref),
    ]
    copies = [pltpu.make_async_copy(source, target, sems.at[i]) for i, (source, target) in enumerate(ends)]
    for copy in copies:
        copy.start()
    odd = jnp.bitwise_and(lax.axis_index("kv"), 1)
    odd = jnp.full((STAT_ROWS, PAGE), odd, jnp.int32).astype(jnp.float32)
    out_ref[ROWS:, PARITY * PAGE : (PARITY + 1) * PAGE] = odd.astype(jnp.bfloat16)
    for copy in copies[:3]:
        copy.wait()
    last = jnp.int32(0)
    for bit in (64, 32, 16, 8, 4, 2, 1):
        last = jnp.where(segments[last + bit] == segments[0], last + bit, last)
    cut = jnp.full((STAT_ROWS, PAGE), last + 1, jnp.int32).astype(jnp.float32)
    out_ref[ROWS:, CUT * PAGE : (CUT + 1) * PAGE] = cut.astype(jnp.bfloat16)
    count0 = lax.shift_right_logical(lengths[0] + (PAGE - 1), 7)
    slot_row = iota(0, (STAT_ROWS, PAGE))
    for block in range(REACH):
        tile = jnp.zeros((STAT_ROWS, PAGE), jnp.int32)
        for k in range(block * PPO, (block + 1) * PPO):
            left0 = jnp.clip(lengths[0] - k * PAGE, 0, PAGE)
            left1 = jnp.clip(lengths[1] - (k - count0) * PAGE, 0, PAGE)
            left = jnp.where(k < count0, left0, -left1)
            tile = jnp.where(slot_row == jnp.bitwise_and(table[0, k], PPO - 1), left, tile)
        out_ref[ROWS:, block * PAGE : (block + 1) * PAGE] = tile.astype(jnp.float32).astype(jnp.bfloat16)
    for copy in copies[3:]:
        copy.wait()


def scores(query, keys):
    return lax.dot_general(query, keys, (((1,), (1,)), ((), ())), preferred_element_type=jnp.float32)


def attend(q_ref, keys, values):
    lanes = segment_lanes(q_ref)

    def group_scores(start):
        query = [jnp.concatenate([head(q_ref, h), lanes], 1) for h in range(start, start + GROUP)]
        return scores(jnp.concatenate(query, 0), keys)

    parts = []
    later = group_scores(0)
    for start in range(0, HEADS, GROUP):
        s = later
        if start + GROUP < HEADS:
            later = group_scores(start + GROUP)
        top = jnp.max(s, axis=1, keepdims=True)
        w = jnp.exp2((s - top) * SCALE2).astype(jnp.bfloat16)
        out = jnp.dot(w, values, preferred_element_type=jnp.float32)
        for i in range(GROUP):
            rows = slice(i * ROWS, (i + 1) * ROWS)
            parts.append((out[rows, :HD], top[rows] * SCALE2, out[rows, HD:]))
    return parts


def join(a, b):
    top = jnp.maximum(a[1], b[1])
    fa, fb = jnp.exp2(a[1] - top), jnp.exp2(b[1] - top)
    return a[0] * fa + b[0] * fb, top, a[2] * fa + b[2] * fb


def head(x, h):
    return x[:ROWS, h * HD : (h + 1) * HD]


def columns(cols):
    lane = iota(1)
    out = jnp.zeros((ROWS, PAGE), jnp.float32)
    for i, col in enumerate(cols):
        out = jnp.where(lane == i, col, out)
    return out


def write_payload(out_ref, parts):
    for h, (o, top, total) in enumerate(parts):
        out_ref[:ROWS, h * HD : (h + 1) * HD] = (o / total).astype(jnp.bfloat16)
    lse = columns([top + jnp.log2(total[:, :1]) for _, top, total in parts]).T[:STAT_ROWS]
    left = lse
    for i in range(3):
        term = left.astype(jnp.bfloat16)
        out_ref[ROWS:, i * HD : (i + 1) * HD] = term
        left = left - term.astype(jnp.float32)
    out_ref[ROWS:, 3 * HD :] = jnp.zeros((STAT_ROWS, WIDTH - 3 * HD), jnp.bfloat16)


def write_partial(out_ref, lse_ref, parts):
    for h, (o, _, total) in enumerate(parts):
        out_ref[:, h * HD : (h + 1) * HD] = o / total
    lse_ref[...] = columns([top + jnp.log2(total[:, :1]) for _, top, total in parts])


def payload_lse(ref):
    lse = jnp.zeros((STAT_ROWS, PAGE), jnp.float32)
    for i in (2, 1, 0):
        lse = lse + ref[ROWS:, i * HD : (i + 1) * HD].astype(jnp.float32)
    full = jnp.concatenate([lse, jnp.zeros((ROWS - STAT_ROWS, PAGE), jnp.float32)], 0)
    return full.T


def near_kernel(q_ref, kv_ref, page_ref, out_ref, lse_ref):
    row, lane = iota(0), iota(1)
    cut = fact(q_ref, CUT)[:1]
    same = (lane <= row) & ((lane.astype(jnp.float32) >= cut) | (row.astype(jnp.float32) < cut))
    bias = jnp.where(same, 0.0, NEGATIVE)
    parts = attend(q_ref, *block_keys(q_ref, page_ref, 0))
    values = jnp.concatenate([kv_ref[:, HD:], jnp.ones((ROWS, HD), jnp.bfloat16)], 1)
    for h in range(HEADS):
        s = scores(head(q_ref, h), kv_ref[:, :HD]) + bias
        top = jnp.max(s, axis=1, keepdims=True)
        w = jnp.exp2((s - top) * SCALE2).astype(jnp.bfloat16)
        out = jnp.dot(w, values, preferred_element_type=jnp.float32)
        parts[h] = join(parts[h], (out[:, :HD], top * SCALE2, out[:, HD:]))
    write_partial(out_ref, lse_ref, parts)


def far_kernel(q_ref, page_ref, out_ref):
    write_payload(out_ref, attend(q_ref, *block_keys(q_ref, page_ref, 3)))


def swap_parts(parity, q_ref, swap_ref, part_ref, part_lse_ref):
    parts = attend(q_ref, *block_keys(q_ref, swap_ref, 1, fact(q_ref, PARITY) != parity))
    given = [(part_ref[:, h * HD : (h + 1) * HD], part_lse_ref[:, h : h + 1], 1.0) for h in range(HEADS)]
    return [join(a, b) for a, b in zip(given, parts)]


def two_kernel(q_ref, page_ref, out_ref, lse_ref):
    write_partial(out_ref, lse_ref, attend(q_ref, *block_keys(q_ref, page_ref, 2)))


def swap_parts(parity, q_ref, swap_ref, part_ref, part_lse_ref):
    parts = attend(q_ref, *block_keys(q_ref, swap_ref, 1, fact(q_ref, PARITY) != parity))
    given = [(part_ref[:, h * HD : (h + 1) * HD], part_lse_ref[:, h : h + 1], 1.0) for h in range(HEADS)]
    return [join(a, b) for a, b in zip(given, parts)]


def middle_kernel(q_ref, page_ref, swap_ref, out_ref):
    pages = block_keys(q_ref, page_ref, 2)
    swapped = block_keys(q_ref, swap_ref, 1, fact(q_ref, PARITY) == 0.0)
    write_payload(out_ref, attend(q_ref, *(jnp.concatenate(both, 0) for both in zip(pages, swapped))))


def middle_kernel(q_ref, swap_ref, part_ref, part_lse_ref, out_ref):
    write_payload(out_ref, swap_parts(1.0, q_ref, swap_ref, part_ref, part_lse_ref))


def own_kernel(q_ref, swap_ref, part_ref, part_lse_ref, out_ref, lse_ref):
    write_partial(out_ref, lse_ref, swap_parts(0.0, q_ref, swap_ref, part_ref, part_lse_ref))


def final_kernel(own_ref, own_lse_ref, two_ref, three_ref, out_ref):
    refs = (own_ref, two_ref, three_ref)
    lses = [own_lse_ref[...], payload_lse(two_ref), payload_lse(three_ref)]
    top = functools.reduce(jnp.maximum, lses)
    shares = [jnp.exp2(x - top) for x in lses]
    total = sum(shares)
    shares = [x / total for x in shares]
    for h in range(HEADS):
        span = slice(h * HD, (h + 1) * HD)
        out = 0.0
        for ref, share in zip(refs, shares):
            out = out + ref[:ROWS, span].astype(jnp.float32) * share[:, h : h + 1]
        out_ref[:, span] = out.astype(jnp.bfloat16)


SMEM = pl.BlockSpec(memory_space=pltpu.SMEM)
VMEM = pl.BlockSpec(memory_space=pltpu.VMEM)


FULL = jax.ShapeDtypeStruct((ROWS, WIDTH), jnp.float32)
LSE = jax.ShapeDtypeStruct((ROWS, PAGE), jnp.float32)
SENT = jax.ShapeDtypeStruct((ROWS + STAT_ROWS, WIDTH), jnp.bfloat16)
RESULT = jax.ShapeDtypeStruct((ROWS, WIDTH), jnp.bfloat16)


def cost(keys):
    return pl.CostEstimate(
        flops=4 * ROWS * HEADS * keys * HD,
        bytes_accessed=4 * keys * HD + 4 * ROWS * WIDTH,
        transcendentals=ROWS * HEADS * keys,
    )


PARAMS = pltpu.CompilerParams(vmem_limit_bytes=16 << 20)


def call(body, name, keys, out_shape, *arrays):
    return pl.pallas_call(
        body,
        in_specs=[VMEM] * len(arrays),
        out_specs=jax.tree.map(lambda _: VMEM, out_shape),
        out_shape=out_shape,
        compiler_params=PARAMS,
        cost_estimate=cost(keys),
        name=name,
    )(*arrays)


def shift(value, steps, count):
    return lax.ppermute(value, AXES, [(s, (s + steps) % count) for s in range(count)])


def after(value, *others):
    return lax.optimization_barrier((value, *others))[0]


def per_device(queries, new_kv, segment_ids, prefix_len, page_table, cache):
    count = lax.axis_size(AXES)
    packed, sent1 = pl.pallas_call(
        pack_kernel,
        in_specs=[pl.BlockSpec(memory_space=pltpu.HBM)] * 5,
        out_specs=[VMEM, VMEM],
        out_shape=[SENT, jax.ShapeDtypeStruct((PPO, PAGE, 2 * HD), jnp.bfloat16)],
        scratch_shapes=[
            pltpu.SMEM(prefix_len.shape, jnp.int32),
            pltpu.SMEM(page_table.shape, jnp.int32),
            pltpu.SMEM(segment_ids.shape, jnp.int32),
            pltpu.SemaphoreType.DMA((5,)),
        ],
        compiler_params=pltpu.CompilerParams(vmem_limit_bytes=16 << 20),
        cost_estimate=cost(16),
        name="pack",
    )(*(pltpu.with_memory_space_constraint(x, pltpu.HBM) for x in (prefix_len, page_table, segment_ids, queries, cache)))
    q3 = shift(packed, 3, count)
    odd_gets = lax.ppermute(sent1, AXES, [(s, s + 1) for s in range(0, count, 2)])
    pool = after(cache, packed)
    blocks = [pool[i * PPO : (i + 1) * PPO] for i in range(REACH)]
    near = call(near_kernel, "near", 8, (FULL, LSE), packed, new_kv, blocks[0])
    q2 = shift(after(packed, near[1]), 2, count)
    even_gets = lax.ppermute(after(sent1, near[1]), AXES, [(s + 1, s) for s in range(0, count, 2)])

    far = call(far_kernel, "far", 1024 * FAR, SENT, q3, blocks[3])
    back3 = shift(far, -3, count)
    two = call(two_kernel, "two", 1024, (FULL, LSE), q2, after(blocks[2], far))
    middle = call(middle_kernel, "middle", 1024, SENT, q2, after(odd_gets, two[1]), *two)
    back2 = shift(middle, -2, count)
    own = call(own_kernel, "own", 1024, (FULL, LSE), packed, even_gets, *near)
    return call(final_kernel, "final", 16, RESULT, *own, back2, back3)


def solution(mesh):
    placed = (
        P(AXES, None),
        P(AXES, None),
        P(AXES),
        P(AXES),
        P(AXES, None),
        P(AXES, None, None),
    )
    return jax.shard_map(per_device, mesh=mesh, in_specs=placed, out_specs=P(AXES, None), check_vma=False)
```

```python
import functools

import jax
import jax.numpy as jnp
from jax import lax
from jax.experimental import pallas as pl
from jax.experimental.pallas import tpu as pltpu
from jax.sharding import PartitionSpec as P

HD = 128
HEADS = 6
PAGE = 128
REACH = 4
PPO = 8
FAR = 2
GROUP = 3
ROWS = 128
WIDTH = HEADS * HD
STAT_ROWS = 8
NEGATIVE = -1e30
SCALE2 = HD**-0.5 * 1.4426950408889634
AXES = ("tok", "kv")
CUT, PARITY = REACH, REACH + 1


def iota(axis, shape=(ROWS, PAGE)):
    return lax.broadcasted_iota(jnp.int32, shape, axis)


def fact(q_ref, tile):
    return q_ref[ROWS:, tile * PAGE : (tile + 1) * PAGE].astype(jnp.float32)


def segment_lanes(q_ref):
    cut = fact(q_ref, CUT)[:1]
    row, lane = iota(0).astype(jnp.float32), iota(1)
    low = jnp.where(lane == 0, 0.0, cut)
    high = jnp.where(lane == 0, cut, jnp.where(lane == 1, float(ROWS), 0.0))
    return jnp.where((row >= low) & (row < high), 1.0, 0.0).astype(jnp.bfloat16)


def block_keys(q_ref, pages, block, skip=None):
    row, lane = iota(0).astype(jnp.float32), iota(1)
    counts = fact(q_ref, block)
    if skip is not None:
        counts = jnp.where(skip, 0.0, counts)
    keys, values = [], []
    ones = jnp.ones((PAGE, PAGE), jnp.bfloat16)
    for slot in range(PPO):
        count = counts[slot : slot + 1]
        count = jnp.where(lane[:1] == 0, count, jnp.where(lane[:1] == 1, -count, float(PAGE)))
        bias = jnp.where(row < count, 0.0, NEGATIVE).astype(jnp.bfloat16)
        page = pages[slot]
        keys.append(jnp.concatenate([page[:, :HD], bias], 1))
        values.append(jnp.concatenate([page[:, HD:], ones], 1))
    return jnp.concatenate(keys, 0), jnp.concatenate(values, 0)


def pack_kernel(length_hbm, table_hbm, segment_hbm, q_hbm, cache_hbm, out_ref, swap_ref, lengths, table, segments, sems):
    ends = [
        (segment_hbm, segments),
        (length_hbm, lengths),
        (table_hbm, table),
        (q_hbm, out_ref.at[:ROWS]),
        (cache_hbm.at[PPO : 2 * PPO], swap_ref),
    ]
    copies = [pltpu.make_async_copy(source, target, sems.at[i]) for i, (source, target) in enumerate(ends)]
    for copy in copies:
        copy.start()
    odd = jnp.bitwise_and(lax.axis_index("kv"), 1)
    odd = jnp.full((STAT_ROWS, PAGE), odd, jnp.int32).astype(jnp.float32)
    out_ref[ROWS:, PARITY * PAGE : (PARITY + 1) * PAGE] = odd.astype(jnp.bfloat16)
    for copy in copies[:3]:
        copy.wait()
    last = jnp.int32(0)
    for bit in (64, 32, 16, 8, 4, 2, 1):
        last = jnp.where(segments[last + bit] == segments[0], last + bit, last)
    cut = jnp.full((STAT_ROWS, PAGE), last + 1, jnp.int32).astype(jnp.float32)
    out_ref[ROWS:, CUT * PAGE : (CUT + 1) * PAGE] = cut.astype(jnp.bfloat16)
    count0 = lax.shift_right_logical(lengths[0] + (PAGE - 1), 7)
    slot_row = iota(0, (STAT_ROWS, PAGE))
    for block in range(REACH):
        tile = jnp.zeros((STAT_ROWS, PAGE), jnp.int32)
        for k in range(block * PPO, (block + 1) * PPO):
            left0 = jnp.clip(lengths[0] - k * PAGE, 0, PAGE)
            left1 = jnp.clip(lengths[1] - (k - count0) * PAGE, 0, PAGE)
            left = jnp.where(k < count0, left0, -left1)
            tile = jnp.where(slot_row == jnp.bitwise_and(table[0, k], PPO - 1), left, tile)
        out_ref[ROWS:, block * PAGE : (block + 1) * PAGE] = tile.astype(jnp.float32).astype(jnp.bfloat16)
    for copy in copies[3:]:
        copy.wait()


def scores(query, keys):
    return lax.dot_general(query, keys, (((1,), (1,)), ((), ())), preferred_element_type=jnp.float32)


def attend(q_ref, keys, values):
    lanes = segment_lanes(q_ref)

    def group_scores(start):
        query = [jnp.concatenate([head(q_ref, h), lanes], 1) for h in range(start, start + GROUP)]
        return scores(jnp.concatenate(query, 0), keys)

    parts = []
    later = group_scores(0)
    for start in range(0, HEADS, GROUP):
        s = later
        if start + GROUP < HEADS:
            later = group_scores(start + GROUP)
        top = jnp.max(s, axis=1, keepdims=True)
        w = jnp.exp2((s - top) * SCALE2).astype(jnp.bfloat16)
        out = jnp.dot(w, values, preferred_element_type=jnp.float32)
        for i in range(GROUP):
            rows = slice(i * ROWS, (i + 1) * ROWS)
            parts.append((out[rows, :HD], top[rows] * SCALE2, out[rows, HD:]))
    return parts


def join(a, b):
    top = jnp.maximum(a[1], b[1])
    fa, fb = jnp.exp2(a[1] - top), jnp.exp2(b[1] - top)
    return a[0] * fa + b[0] * fb, top, a[2] * fa + b[2] * fb


def head(x, h):
    return x[:ROWS, h * HD : (h + 1) * HD]


def columns(cols):
    lane = iota(1)
    out = jnp.zeros((ROWS, PAGE), jnp.float32)
    for i, col in enumerate(cols):
        out = jnp.where(lane == i, col, out)
    return out


def write_payload(out_ref, parts):
    for h, (o, top, total) in enumerate(parts):
        out_ref[:ROWS, h * HD : (h + 1) * HD] = (o / total).astype(jnp.bfloat16)
    lse = columns([top + jnp.log2(total[:, :1]) for _, top, total in parts]).T[:STAT_ROWS]
    left = lse
    for i in range(3):
        term = left.astype(jnp.bfloat16)
        out_ref[ROWS:, i * HD : (i + 1) * HD] = term
        left = left - term.astype(jnp.float32)
    out_ref[ROWS:, 3 * HD :] = jnp.zeros((STAT_ROWS, WIDTH - 3 * HD), jnp.bfloat16)


def write_partial(out_ref, lse_ref, parts):
    for h, (o, top, total) in enumerate(parts):
        out_ref[:, h * HD : (h + 1) * HD] = o / total
        lse_ref[:, h * HD : (h + 1) * HD] = top + jnp.log2(total)


def payload_lse(ref):
    lse = jnp.zeros((STAT_ROWS, PAGE), jnp.float32)
    for i in (2, 1, 0):
        lse = lse + ref[ROWS:, i * HD : (i + 1) * HD].astype(jnp.float32)
    full = jnp.concatenate([lse, jnp.zeros((ROWS - STAT_ROWS, PAGE), jnp.float32)], 0)
    return full.T


def near_kernel(q_ref, kv_ref, page_ref, out_ref, lse_ref):
    row, lane = iota(0), iota(1)
    cut = fact(q_ref, CUT)[:1]
    same = (lane <= row) & ((lane.astype(jnp.float32) >= cut) | (row.astype(jnp.float32) < cut))
    bias = jnp.where(same, 0.0, NEGATIVE)
    parts = attend(q_ref, *block_keys(q_ref, page_ref, 0))
    values = jnp.concatenate([kv_ref[:, HD:], jnp.ones((ROWS, HD), jnp.bfloat16)], 1)
    for h in range(HEADS):
        s = scores(head(q_ref, h), kv_ref[:, :HD]) + bias
        top = jnp.max(s, axis=1, keepdims=True)
        w = jnp.exp2((s - top) * SCALE2).astype(jnp.bfloat16)
        out = jnp.dot(w, values, preferred_element_type=jnp.float32)
        parts[h] = join(parts[h], (out[:, :HD], top * SCALE2, out[:, HD:]))
    write_partial(out_ref, lse_ref, parts)


def far_kernel(q_ref, page_ref, out_ref):
    write_payload(out_ref, attend(q_ref, *block_keys(q_ref, page_ref, 3)))


def swap_parts(parity, q_ref, swap_ref, part_ref, part_lse_ref):
    parts = attend(q_ref, *block_keys(q_ref, swap_ref, 1, fact(q_ref, PARITY) != parity))
    spans = [slice(h * HD, (h + 1) * HD) for h in range(HEADS)]
    given = [(part_ref[:, span], part_lse_ref[:, span], 1.0) for span in spans]
    return [join(a, b) for a, b in zip(given, parts)]


def two_kernel(q_ref, page_ref, out_ref, lse_ref):
    write_partial(out_ref, lse_ref, attend(q_ref, *block_keys(q_ref, page_ref, 2)))


def swap_parts(parity, q_ref, swap_ref, part_ref, part_lse_ref):
    parts = attend(q_ref, *block_keys(q_ref, swap_ref, 1, fact(q_ref, PARITY) != parity))
    spans = [slice(h * HD, (h + 1) * HD) for h in range(HEADS)]
    given = [(part_ref[:, span], part_lse_ref[:, span], 1.0) for span in spans]
    return [join(a, b) for a, b in zip(given, parts)]


def middle_kernel(q_ref, page_ref, swap_ref, out_ref):
    pages = block_keys(q_ref, page_ref, 2)
    swapped = block_keys(q_ref, swap_ref, 1, fact(q_ref, PARITY) == 0.0)
    write_payload(out_ref, attend(q_ref, *(jnp.concatenate(both, 0) for both in zip(pages, swapped))))


def middle_kernel(q_ref, swap_ref, part_ref, part_lse_ref, out_ref):
    write_payload(out_ref, swap_parts(1.0, q_ref, swap_ref, part_ref, part_lse_ref))


def own_kernel(q_ref, swap_ref, part_ref, part_lse_ref, out_ref, lse_ref):
    parts = swap_parts(0.0, q_ref, swap_ref, part_ref, part_lse_ref)
    for h, (o, _, total) in enumerate(parts):
        out_ref[:, h * HD : (h + 1) * HD] = o / total
    lse_ref[...] = columns([top + jnp.log2(total) for _, top, total in parts])


def final_kernel(own_ref, own_lse_ref, two_ref, three_ref, out_ref):
    refs = (own_ref, two_ref, three_ref)
    lses = [own_lse_ref[...], payload_lse(two_ref), payload_lse(three_ref)]
    top = functools.reduce(jnp.maximum, lses)
    shares = [jnp.exp2(x - top) for x in lses]
    total = sum(shares)
    shares = [x / total for x in shares]
    for h in range(HEADS):
        span = slice(h * HD, (h + 1) * HD)
        out = 0.0
        for ref, share in zip(refs, shares):
            out = out + ref[:ROWS, span].astype(jnp.float32) * share[:, h : h + 1]
        out_ref[:, span] = out.astype(jnp.bfloat16)


SMEM = pl.BlockSpec(memory_space=pltpu.SMEM)
VMEM = pl.BlockSpec(memory_space=pltpu.VMEM)


FULL = jax.ShapeDtypeStruct((ROWS, WIDTH), jnp.float32)
LSE = jax.ShapeDtypeStruct((ROWS, PAGE), jnp.float32)
SENT = jax.ShapeDtypeStruct((ROWS + STAT_ROWS, WIDTH), jnp.bfloat16)
RESULT = jax.ShapeDtypeStruct((ROWS, WIDTH), jnp.bfloat16)


def cost(keys):
    return pl.CostEstimate(
        flops=4 * ROWS * HEADS * keys * HD,
        bytes_accessed=4 * keys * HD + 4 * ROWS * WIDTH,
        transcendentals=ROWS * HEADS * keys,
    )


PARAMS = pltpu.CompilerParams(vmem_limit_bytes=16 << 20)


def call(body, name, keys, out_shape, *arrays):
    return pl.pallas_call(
        body,
        in_specs=[VMEM] * len(arrays),
        out_specs=jax.tree.map(lambda _: VMEM, out_shape),
        out_shape=out_shape,
        compiler_params=PARAMS,
        cost_estimate=cost(keys),
        name=name,
    )(*arrays)


def shift(value, steps, count):
    return lax.ppermute(value, AXES, [(s, (s + steps) % count) for s in range(count)])


def after(value, *others):
    return lax.optimization_barrier((value, *others))[0]


def per_device(queries, new_kv, segment_ids, prefix_len, page_table, cache):
    count = lax.axis_size(AXES)
    packed, sent1 = pl.pallas_call(
        pack_kernel,
        in_specs=[pl.BlockSpec(memory_space=pltpu.HBM)] * 5,
        out_specs=[VMEM, VMEM],
        out_shape=[SENT, jax.ShapeDtypeStruct((PPO, PAGE, 2 * HD), jnp.bfloat16)],
        scratch_shapes=[
            pltpu.SMEM(prefix_len.shape, jnp.int32),
            pltpu.SMEM(page_table.shape, jnp.int32),
            pltpu.SMEM(segment_ids.shape, jnp.int32),
            pltpu.SemaphoreType.DMA((5,)),
        ],
        compiler_params=pltpu.CompilerParams(vmem_limit_bytes=16 << 20),
        cost_estimate=cost(16),
        name="pack",
    )(*(pltpu.with_memory_space_constraint(x, pltpu.HBM) for x in (prefix_len, page_table, segment_ids, queries, cache)))
    q3 = shift(packed, 3, count)
    odd_gets = lax.ppermute(sent1, AXES, [(s, s + 1) for s in range(0, count, 2)])
    pool = after(cache, packed)
    blocks = [pool[i * PPO : (i + 1) * PPO] for i in range(REACH)]
    near = call(near_kernel, "near", 8, (FULL, FULL), packed, new_kv, blocks[0])
    q2 = shift(after(packed, near[1]), 2, count)
    even_gets = lax.ppermute(after(sent1, near[1]), AXES, [(s + 1, s) for s in range(0, count, 2)])

    far = call(far_kernel, "far", 1024 * FAR, SENT, q3, blocks[3])
    back3 = shift(far, -3, count)
    two = call(two_kernel, "two", 1024, (FULL, FULL), q2, after(blocks[2], far))
    middle = call(middle_kernel, "middle", 1024, SENT, q2, after(odd_gets, two[1]), *two)
    back2 = shift(middle, -2, count)
    own = call(own_kernel, "own", 1024, (FULL, LSE), packed, even_gets, *near)
    return call(final_kernel, "final", 16, RESULT, *own, back2, back3)


def solution(mesh):
    placed = (
        P(AXES, None),
        P(AXES, None),
        P(AXES),
        P(AXES),
        P(AXES, None),
        P(AXES, None, None),
    )
    return jax.shard_map(per_device, mesh=mesh, in_specs=placed, out_specs=P(AXES, None), check_vma=False)
```

```python
import functools

import jax
import jax.numpy as jnp
from jax import lax
from jax.experimental import pallas as pl
from jax.experimental.pallas import tpu as pltpu
from jax.sharding import PartitionSpec as P

HD = 128
HEADS = 6
PAGE = 128
REACH = 4
PPO = 8
FAR = 2
GROUP = 3
ROWS = 128
WIDTH = HEADS * HD
STAT_ROWS = 8
NEGATIVE = -1e30
SCALE2 = HD**-0.5 * 1.4426950408889634
AXES = ("tok", "kv")
CUT, PARITY = REACH, REACH + 1


def iota(axis, shape=(ROWS, PAGE)):
    return lax.broadcasted_iota(jnp.int32, shape, axis)


def fact(q_ref, tile):
    return q_ref[ROWS:, tile * PAGE : (tile + 1) * PAGE].astype(jnp.float32)


def segment_lanes(q_ref):
    cut = fact(q_ref, CUT)[:1]
    row, lane = iota(0).astype(jnp.float32), iota(1)
    low = jnp.where(lane == 0, 0.0, cut)
    high = jnp.where(lane == 0, cut, jnp.where(lane == 1, float(ROWS), 0.0))
    return jnp.where((row >= low) & (row < high), 1.0, 0.0).astype(jnp.bfloat16)


def block_keys(q_ref, pages, block, skip=None):
    row, lane = iota(0).astype(jnp.float32), iota(1)
    counts = fact(q_ref, block)
    if skip is not None:
        counts = jnp.where(skip, 0.0, counts)
    keys, values = [], []
    ones = jnp.ones((PAGE, PAGE), jnp.bfloat16)
    for slot in range(PPO):
        count = counts[slot : slot + 1]
        count = jnp.where(lane[:1] == 0, count, jnp.where(lane[:1] == 1, -count, float(PAGE)))
        bias = jnp.where(row < count, 0.0, NEGATIVE).astype(jnp.bfloat16)
        page = pages[slot]
        keys.append(jnp.concatenate([page[:, :HD], bias], 1))
        values.append(jnp.concatenate([page[:, HD:], ones], 1))
    return jnp.concatenate(keys, 0), jnp.concatenate(values, 0)


def pack_kernel(length_hbm, table_hbm, segment_hbm, q_hbm, cache_hbm, out_ref, swap_ref, lengths, table, segments, sems):
    ends = [
        (segment_hbm, segments),
        (length_hbm, lengths),
        (table_hbm, table),
        (q_hbm, out_ref.at[:ROWS]),
        (cache_hbm.at[PPO : 2 * PPO], swap_ref),
    ]
    copies = [pltpu.make_async_copy(source, target, sems.at[i]) for i, (source, target) in enumerate(ends)]
    for copy in copies:
        copy.start()
    odd = jnp.bitwise_and(lax.axis_index("kv"), 1)
    odd = jnp.full((STAT_ROWS, PAGE), odd, jnp.int32).astype(jnp.float32)
    out_ref[ROWS:, PARITY * PAGE : (PARITY + 1) * PAGE] = odd.astype(jnp.bfloat16)
    for copy in copies[:3]:
        copy.wait()
    last = jnp.int32(0)
    for bit in (64, 32, 16, 8, 4, 2, 1):
        last = jnp.where(segments[last + bit] == segments[0], last + bit, last)
    cut = jnp.full((STAT_ROWS, PAGE), last + 1, jnp.int32).astype(jnp.float32)
    out_ref[ROWS:, CUT * PAGE : (CUT + 1) * PAGE] = cut.astype(jnp.bfloat16)
    count0 = lax.shift_right_logical(lengths[0] + (PAGE - 1), 7)
    slot_row = iota(0, (STAT_ROWS, PAGE))
    for block in range(REACH):
        tile = jnp.zeros((STAT_ROWS, PAGE), jnp.int32)
        for k in range(block * PPO, (block + 1) * PPO):
            left0 = jnp.clip(lengths[0] - k * PAGE, 0, PAGE)
            left1 = jnp.clip(lengths[1] - (k - count0) * PAGE, 0, PAGE)
            left = jnp.where(k < count0, left0, -left1)
            tile = jnp.where(slot_row == jnp.bitwise_and(table[0, k], PPO - 1), left, tile)
        out_ref[ROWS:, block * PAGE : (block + 1) * PAGE] = tile.astype(jnp.float32).astype(jnp.bfloat16)
    for copy in copies[3:]:
        copy.wait()


def scores(query, keys):
    return lax.dot_general(query, keys, (((1,), (1,)), ((), ())), preferred_element_type=jnp.float32)


def attend(q_ref, keys, values):
    lanes = segment_lanes(q_ref)

    def group_scores(start):
        query = [jnp.concatenate([head(q_ref, h), lanes], 1) for h in range(start, start + GROUP)]
        return scores(jnp.concatenate(query, 0), keys)

    parts = []
    later = group_scores(0)
    for start in range(0, HEADS, GROUP):
        s = later
        if start + GROUP < HEADS:
            later = group_scores(start + GROUP)
        top = jnp.max(s, axis=1, keepdims=True)
        w = jnp.exp2((s - top) * SCALE2).astype(jnp.bfloat16)
        out = jnp.dot(w, values, preferred_element_type=jnp.float32)
        for i in range(GROUP):
            rows = slice(i * ROWS, (i + 1) * ROWS)
            parts.append((out[rows, :HD], top[rows] * SCALE2, out[rows, HD:]))
    return parts


def join(a, b):
    top = jnp.maximum(a[1], b[1])
    fa, fb = jnp.exp2(a[1] - top), jnp.exp2(b[1] - top)
    return a[0] * fa + b[0] * fb, top, a[2] * fa + b[2] * fb


def head(x, h):
    return x[:ROWS, h * HD : (h + 1) * HD]


def columns(cols):
    lane = iota(1)
    out = jnp.zeros((ROWS, PAGE), jnp.float32)
    for i, col in enumerate(cols):
        out = jnp.where(lane == i, col, out)
    return out


def write_payload(out_ref, parts):
    for h, (o, top, total) in enumerate(parts):
        out_ref[:ROWS, h * HD : (h + 1) * HD] = (o / total).astype(jnp.bfloat16)
    lse = columns([top + jnp.log2(total[:, :1]) for _, top, total in parts]).T[:STAT_ROWS]
    left = lse
    for i in range(3):
        term = left.astype(jnp.bfloat16)
        out_ref[ROWS:, i * HD : (i + 1) * HD] = term
        left = left - term.astype(jnp.float32)
    out_ref[ROWS:, 3 * HD :] = jnp.zeros((STAT_ROWS, WIDTH - 3 * HD), jnp.bfloat16)


def write_partial(out_ref, lse_ref, parts):
    for h, (o, top, total) in enumerate(parts):
        out_ref[:, h * HD : (h + 1) * HD] = o / total
        lse_ref[:, h * HD : (h + 1) * HD] = top + jnp.log2(total)


def payload_lse(ref):
    lse = jnp.zeros((STAT_ROWS, PAGE), jnp.float32)
    for i in (2, 1, 0):
        lse = lse + ref[ROWS:, i * HD : (i + 1) * HD].astype(jnp.float32)
    full = jnp.concatenate([lse, jnp.zeros((ROWS - STAT_ROWS, PAGE), jnp.float32)], 0)
    return full.T


def near_kernel(q_ref, kv_ref, page_ref, out_ref, lse_ref):
    row, lane = iota(0), iota(1)
    cut = fact(q_ref, CUT)[:1]
    same = (lane <= row) & ((lane.astype(jnp.float32) >= cut) | (row.astype(jnp.float32) < cut))
    bias = jnp.where(same, 0.0, NEGATIVE)
    parts = attend(q_ref, *block_keys(q_ref, page_ref, 0))
    values = jnp.concatenate([kv_ref[:, HD:], jnp.ones((ROWS, HD), jnp.bfloat16)], 1)
    for h in range(HEADS):
        s = scores(head(q_ref, h), kv_ref[:, :HD]) + bias
        top = jnp.max(s, axis=1, keepdims=True)
        w = jnp.exp2((s - top) * SCALE2).astype(jnp.bfloat16)
        out = jnp.dot(w, values, preferred_element_type=jnp.float32)
        parts[h] = join(parts[h], (out[:, :HD], top * SCALE2, out[:, HD:]))
    write_partial(out_ref, lse_ref, parts)


def far_kernel(q_ref, page_ref, out_ref):
    write_payload(out_ref, attend(q_ref, *block_keys(q_ref, page_ref, 3)))


def swap_parts(parity, q_ref, swap_ref, part_ref, part_lse_ref):
    parts = attend(q_ref, *block_keys(q_ref, swap_ref, 1, fact(q_ref, PARITY) != parity))
    spans = [slice(h * HD, (h + 1) * HD) for h in range(HEADS)]
    given = [(part_ref[:, span], part_lse_ref[:, span], 1.0) for span in spans]
    return [join(a, b) for a, b in zip(given, parts)]


def two_kernel(q_ref, page_ref, out_ref, lse_ref):
    write_partial(out_ref, lse_ref, attend(q_ref, *block_keys(q_ref, page_ref, 2)))


def swap_parts(parity, q_ref, swap_ref, part_ref, part_lse_ref):
    parts = attend(q_ref, *block_keys(q_ref, swap_ref, 1, fact(q_ref, PARITY) != parity))
    spans = [slice(h * HD, (h + 1) * HD) for h in range(HEADS)]
    given = [(part_ref[:, span], part_lse_ref[:, span], 1.0) for span in spans]
    return [join(a, b) for a, b in zip(given, parts)]


def middle_kernel(q_ref, swap_ref, part_ref, part_lse_ref, out_ref):
    odd = jnp.bitwise_and(lax.axis_index("kv"), 1) == 1

    @pl.when(odd)
    def _():
        write_payload(out_ref, swap_parts(1.0, q_ref, swap_ref, part_ref, part_lse_ref))

    @pl.when(jnp.logical_not(odd))
    def _():
        spans = [slice(h * HD, (h + 1) * HD) for h in range(HEADS)]
        one = jnp.ones((ROWS, HD), jnp.float32)
        write_payload(out_ref, [(part_ref[:, span], part_lse_ref[:, span][:, :1], one) for span in spans])


def own_kernel(q_ref, swap_ref, part_ref, part_lse_ref, out_ref, lse_ref):
    parts = swap_parts(0.0, q_ref, swap_ref, part_ref, part_lse_ref)
    for h, (o, _, total) in enumerate(parts):
        out_ref[:, h * HD : (h + 1) * HD] = o / total
    lse_ref[...] = columns([top + jnp.log2(total) for _, top, total in parts])


def final_kernel(own_ref, own_lse_ref, two_ref, three_ref, out_ref):
    refs = (own_ref, two_ref, three_ref)
    lses = [own_lse_ref[...], payload_lse(two_ref), payload_lse(three_ref)]
    top = functools.reduce(jnp.maximum, lses)
    shares = [jnp.exp2(x - top) for x in lses]
    total = sum(shares)
    shares = [x / total for x in shares]
    for h in range(HEADS):
        span = slice(h * HD, (h + 1) * HD)
        out = 0.0
        for ref, share in zip(refs, shares):
            out = out + ref[:ROWS, span].astype(jnp.float32) * share[:, h : h + 1]
        out_ref[:, span] = out.astype(jnp.bfloat16)


SMEM = pl.BlockSpec(memory_space=pltpu.SMEM)
VMEM = pl.BlockSpec(memory_space=pltpu.VMEM)


FULL = jax.ShapeDtypeStruct((ROWS, WIDTH), jnp.float32)
LSE = jax.ShapeDtypeStruct((ROWS, PAGE), jnp.float32)
SENT = jax.ShapeDtypeStruct((ROWS + STAT_ROWS, WIDTH), jnp.bfloat16)
RESULT = jax.ShapeDtypeStruct((ROWS, WIDTH), jnp.bfloat16)


def cost(keys):
    return pl.CostEstimate(
        flops=4 * ROWS * HEADS * keys * HD,
        bytes_accessed=4 * keys * HD + 4 * ROWS * WIDTH,
        transcendentals=ROWS * HEADS * keys,
    )


PARAMS = pltpu.CompilerParams(vmem_limit_bytes=16 << 20)


def call(body, name, keys, out_shape, *arrays):
    return pl.pallas_call(
        body,
        in_specs=[VMEM] * len(arrays),
        out_specs=jax.tree.map(lambda _: VMEM, out_shape),
        out_shape=out_shape,
        compiler_params=PARAMS,
        cost_estimate=cost(keys),
        name=name,
    )(*arrays)


def shift(value, steps, count):
    return lax.ppermute(value, AXES, [(s, (s + steps) % count) for s in range(count)])


def after(value, *others):
    return lax.optimization_barrier((value, *others))[0]


def per_device(queries, new_kv, segment_ids, prefix_len, page_table, cache):
    count = lax.axis_size(AXES)
    packed, sent1 = pl.pallas_call(
        pack_kernel,
        in_specs=[pl.BlockSpec(memory_space=pltpu.HBM)] * 5,
        out_specs=[VMEM, VMEM],
        out_shape=[SENT, jax.ShapeDtypeStruct((PPO, PAGE, 2 * HD), jnp.bfloat16)],
        scratch_shapes=[
            pltpu.SMEM(prefix_len.shape, jnp.int32),
            pltpu.SMEM(page_table.shape, jnp.int32),
            pltpu.SMEM(segment_ids.shape, jnp.int32),
            pltpu.SemaphoreType.DMA((5,)),
        ],
        compiler_params=pltpu.CompilerParams(vmem_limit_bytes=16 << 20),
        cost_estimate=cost(16),
        name="pack",
    )(*(pltpu.with_memory_space_constraint(x, pltpu.HBM) for x in (prefix_len, page_table, segment_ids, queries, cache)))
    q3 = shift(packed, 3, count)
    odd_gets = lax.ppermute(sent1, AXES, [(s, s + 1) for s in range(0, count, 2)])
    pool = after(cache, packed)
    blocks = [pool[i * PPO : (i + 1) * PPO] for i in range(REACH)]
    near = call(near_kernel, "near", 8, (FULL, FULL), packed, new_kv, blocks[0])
    q2 = shift(after(packed, near[1]), 2, count)
    even_gets = lax.ppermute(after(sent1, near[1]), AXES, [(s + 1, s) for s in range(0, count, 2)])

    far = call(far_kernel, "far", 1024 * FAR, SENT, q3, blocks[3])
    back3 = shift(far, -3, count)
    two = call(two_kernel, "two", 1024, (FULL, FULL), q2, after(blocks[2], far))
    middle = call(middle_kernel, "middle", 1024, SENT, q2, after(odd_gets, two[1]), *two)
    back2 = shift(middle, -2, count)
    own = call(own_kernel, "own", 1024, (FULL, LSE), packed, even_gets, *near)
    return call(final_kernel, "final", 16, RESULT, *own, back2, back3)


def solution(mesh):
    placed = (
        P(AXES, None),
        P(AXES, None),
        P(AXES),
        P(AXES),
        P(AXES, None),
        P(AXES, None, None),
    )
    return jax.shard_map(per_device, mesh=mesh, in_specs=placed, out_specs=P(AXES, None), check_vma=False)
```
